32 devices in a mesh: groups: 2 (over x), tensor: 16 (over z, y, core).
Axes of the slice: x: 2, y: 2, z: 4, core: 2. Of those that a mesh axis runs over, the one named last changes fastest.
Arguments:
- teacher_in: bfloat16 [1024, 5376], P(('groups', 'tensor')), parts along dimension 0, may hold values from -6 to 6
- gate_weight: bfloat16 [21504, 5376], P('tensor'), may hold values from -0.078125 to 0.078125
- up_weight: bfloat16 [21504, 5376], P('tensor'), may hold values from -0.078125 to 0.078125
- down_weight: bfloat16 [21504, 5376], P('tensor'), may hold values from -0.0546875 to 0.0546875
- post_gain: bfloat16 [5376], replicated, may hold values from 0.099609375 to 1.8984375
- student_in: bfloat16 [1024, 2560], P(('groups', 'tensor')), parts along dimension 0, may hold values from -6 to 6
- proj_weight: bfloat16 [5376, 2560], P('tensor'), may hold values from -0.125 to 0.125
Outputs:
- loss_value: float32 [2], P('groups'), parts along dimension 0
- proj_grad: float32 [10752, 2560], P(('groups', 'tensor')), parts along dimension 0
- student_grad: bfloat16 [1024, 2560], P(('groups', 'tensor')), parts along dimension 0
The draws below stay inside these ranges and needn't reach their ends.
There are 2 independent parts, one for each index of `groups`. The reference program is written for one: setup_inputs(seed, part) draws one part's arguments, and reference() takes and returns one part's arrays. A program takes and returns all parts, laid end to end along the dimension named above; an argument that names none is the same for every part. Nothing has to cross between parts.
All inputs are finite; a program needn't handle non-finite values.
Results may differ from the reference program's by a relative error of at most 0.0051.
Values may be sent and summed in bfloat16 or wider, within the bound.
A program may use at most 128 MiB of HBM per device.

```python
import jax
import jax.numpy as jnp
from jax import lax

D_T = 5376
FF = 21504
D_S = 2560
TOKENS = 512


def raised(drawn, key, source, target, parts, factor):
    owner, partner = [(jnp.arange(drawn.shape[dim]) // (drawn.shape[dim] // parts)).reshape([-1 if axis == dim else 1 for axis in range(drawn.ndim)]) for dim in (source, target)]
    chosen = jax.random.permutation(key, parts)[partner]
    strong = (owner == chosen) | (owner == (partner + parts // 2) % parts)
    return jnp.where(strong, factor * drawn, drawn)


def block_scale(stream_key, shape, cuts, low, high):
    def one(axis_at, blocks):
        heights = jax.random.uniform(jax.random.fold_in(jax.random.fold_in(stream_key, 6), axis_at), (blocks,), jnp.float32, low / len(cuts), high / len(cuts))
        return jnp.repeat(jnp.exp(heights), shape[axis_at] // blocks).reshape((-1,) + (1,) * (len(shape) - axis_at - 1))

    loudness = one(*cuts[0])
    for cut in cuts[1:]:
        loudness = loudness * one(*cut)
    return loudness


def noise(stream_key, shape, deviation, limit, pieces=(), kind=jnp.bfloat16):
    drawn = deviation * jax.random.normal(stream_key, shape, jnp.float32)
    if pieces:
        drawn = drawn * block_scale(stream_key, shape, pieces, -0.22, 0.18)
    return jnp.clip(drawn, -limit, limit).astype(kind)


def heavy_noise(stream_key, extent, width, reach, cuts, heavy, held_as=jnp.bfloat16):
    drawn = width * jax.random.normal(stream_key, extent, jnp.float32)
    if cuts:
        drawn = drawn * block_scale(stream_key, extent, cuts, -0.22, 0.18)
    return jnp.clip(raised(drawn, jax.random.fold_in(stream_key, 3), *heavy), -reach, reach).astype(held_as)


def setup_inputs(seed: int = 0, part: int = 0) -> dict:
    streams_of = jax.random.split(jax.random.key(seed), 8)
    part_splits = jax.random.split(jax.random.fold_in(streams_of[7], part), 8)
    teacher_in = noise(part_splits[0], (TOKENS, D_T), 1.0, 6.0, ((0, 16),))
    gate_weight = noise(streams_of[1], (FF, D_T), D_T ** -0.5, 0.078125, ((0, 16),))
    up_weight = noise(streams_of[2], (FF, D_T), D_T ** -0.5, 0.078125, ((0, 16),))
    down_weight = heavy_noise(streams_of[3], (FF, D_T), FF ** -0.5, 0.0546875, ((0, 16),), (0, 1, 16, 2.0))
    post_gain = jnp.clip(1.0 + 0.18 * jax.random.normal(streams_of[4], (D_T,), jnp.float32), 0.099609375, 1.8984375).astype(jnp.bfloat16)
    student_in = noise(part_splits[5], (TOKENS, D_S), 1.0, 6.0, ((0, 16),))
    proj_weight = noise(streams_of[6], (D_T, D_S), D_S ** -0.5, 0.125, ((0, 16),))
    return {"teacher_in": teacher_in, "gate_weight": gate_weight, "up_weight": up_weight, "down_weight": down_weight, "post_gain": post_gain, "student_in": student_in, "proj_weight": proj_weight}


def reference(teacher_in, gate_weight, up_weight, down_weight, post_gain, student_in, proj_weight):
    dims = (((1,), (1,)), ((), ()))
    gate_value = lax.dot_general(teacher_in, gate_weight, dims, preferred_element_type=jnp.float32)
    lift_value = lax.dot_general(teacher_in, up_weight, dims, preferred_element_type=jnp.float32)
    hidden = (jax.nn.gelu(gate_value, approximate=True) * lift_value).astype(jnp.bfloat16)
    ffn_out = jnp.dot(hidden, down_weight, preferred_element_type=jnp.float32)
    inv_norm = lax.rsqrt(lax.optimization_barrier(jnp.mean(ffn_out * ffn_out, axis=-1, keepdims=True)) + 1e-06)
    normed = ffn_out * inv_norm * post_gain.astype(jnp.float32)
    target = (teacher_in.astype(jnp.float32) + normed).astype(jnp.bfloat16)
    projected = lax.dot_general(student_in, proj_weight, dims, preferred_element_type=jnp.float32)
    difference = projected - target.astype(jnp.float32)
    loss_value = jnp.sum(difference * difference) / (TOKENS * D_T)
    cotangent = difference.astype(jnp.bfloat16)
    proj_grad = lax.dot_general(cotangent, student_in, (((0,), (0,)), ((), ())), preferred_element_type=jnp.float32)
    student_grad = jnp.dot(cotangent, proj_weight, preferred_element_type=jnp.float32).astype(jnp.bfloat16)
    return (jnp.reshape(loss_value, (1,)), proj_grad, student_grad)
```

```python
import functools

import jax
import jax.numpy as jnp
from jax import lax
from jax.experimental import pallas as pl
from jax.experimental.pallas import tpu as pltpu
from jax.sharding import PartitionSpec as P

epsilon = 1e-06
MESH = pl.DeviceIdType.MESH


def send(src, dst, send_sem, recv_sem, target):
    return pltpu.make_async_remote_copy(
        src_ref=src,
        dst_ref=dst,
        send_sem=send_sem,
        recv_sem=recv_sem,
        device_id={"tensor": target},
        device_id_type=MESH,
    )


def meet(targets):
    barrier = pltpu.get_barrier_semaphore()
    for target in targets:
        pl.semaphore_signal(barrier, inc=1, device_id={"tensor": target}, device_id_type=MESH)
    pl.semaphore_wait(barrier, len(targets))


def position(Z):
    me = lax.axis_index("tensor")
    c = lax.rem(me, 2)
    y = lax.rem(me // 2, 2)
    z = me // 4
    core = me + 1 - 2 * c
    across = me + 2 - 4 * y
    line = [lax.rem(z + k, Z) for k in range(1, Z)]
    return me, c, y, z, core, across, line


def scatter_kernel(Z, J, n, sub, with_loss, *refs):
    if with_loss:
        (lhs, w, part, out, total, wbuf, p, r1, s1, r2, s2, r3, wsem,
         cs, cr, ys, yr, zs, zr, heard, hs, hr) = refs
    else:
        (lhs, w, out, wbuf, p, r1, s1, r2, s2, r3, wsem, cs, cr, ys, yr, zs, zr) = refs
    f32 = jnp.float32
    me, c, y, z, core, across, line = position(Z)
    T = 4 * Z
    B = out.shape[0]

    def fetch(j):
        return pltpu.make_async_copy(w.at[:, pl.ds(j * n, n)], wbuf.at[j % 2], wsem.at[j % 2])

    fetch(0).start()
    others = [lax.rem(me + k, T) for k in range(1, T)]
    meet(others if with_loss else [core, across] + [v * 4 + y * 2 + c for v in line])
    notes = []
    if with_loss:
        for k in range(T - 1):
            notes.append(send(part, heard.at[k], hs.at[k], hr.at[k], others[k]))
            notes[-1].start()

    first = [send(p.at[j, :, :, 1 - c], r1.at[j], cs.at[j], cr.at[j], core) for j in range(J)]
    second = [send(s1.at[j], r2.at[j], ys.at[j], yr.at[j], across) for j in range(J)]
    third = [
        [
            send(s2.at[j, v], r3.at[j, k], zs.at[j, k], zr.at[j, k], v * 4 + y * 2 + c)
            for k, v in enumerate(line)
        ]
        for j in range(J)
    ]

    for t in range(J + 3):
        if t < J:
            fetch(t).wait()
            if t + 1 < J:
                fetch(t + 1).start()

            @pl.loop(0, n // sub)
            def _(i, t=t):
                cols = pl.ds(pl.multiple_of(i * sub, sub), sub)
                got = jnp.dot(lhs[...], wbuf[t % 2, :, cols], preferred_element_type=f32)
                p[t, :, :, :, :, cols] = got.astype(jnp.bfloat16).reshape(Z, 2, 2, B, sub)

            first[t].start()
        j = t - 1
        if 0 <= j < J:
            first[j].wait_recv()
            s1[j] = (p[j, :, 1 - y, c].astype(f32) + r1[j, :, 1 - y].astype(f32)).astype(jnp.bfloat16)
            second[j].start()
        j = t - 2
        if 0 <= j < J:
            second[j].wait_recv()
            s2[j] = (
                p[j, :, y, c].astype(f32) + r1[j, :, y].astype(f32) + r2[j].astype(f32)
            ).astype(jnp.bfloat16)
            for copy in third[j]:
                copy.start()
        j = t - 3
        if 0 <= j < J:
            own = p[j, z, y, c].astype(f32) + r1[j, z, y].astype(f32) + r2[j, z].astype(f32)
            for k, copy in enumerate(third[j]):
                copy.wait_recv()
                own += r3[j, k].astype(f32)
            out[:, j * n : (j + 1) * n] = own.astype(out.dtype)
    for j in range(J):
        first[j].wait_send()
        second[j].wait_send()
        for copy in third[j]:
            copy.wait_send()
    if with_loss:
        acc = part[...]
        for k, copy in enumerate(notes):
            copy.wait()
            acc += heard[k]
        total[...] = acc


def scatter_matmul(lhs, w, T, n, sub, dtype, name, cid, part=None):
    Z = T // 4
    rows, K = lhs.shape
    N = w.shape[1]
    J, B = N // n, rows // T
    bf = jnp.bfloat16
    V = pltpu.VMEM
    D = pltpu.SemaphoreType.DMA
    vm = pl.BlockSpec(memory_space=pltpu.VMEM)
    with_loss = part is not None
    scratch = [
        V((2, K, n), bf), V((J, Z, 2, 2, B, n), bf), V((J, Z, 2, B, n), bf), V((J, Z, B, n), bf),
        V((J, Z, B, n), bf), V((J, Z, B, n), bf), V((J, Z - 1, B, n), bf), D((2,)),
        D((J,)), D((J,)), D((J,)), D((J,)), D((J, Z - 1)), D((J, Z - 1)),
    ]
    outs = [jax.ShapeDtypeStruct((B, N), dtype)]
    args = [lhs, w]
    specs = [vm, pl.BlockSpec(memory_space=pl.ANY)]
    if with_loss:
        scratch += [V((T - 1, 8, 128), jnp.float32), D((T - 1,)), D((T - 1,))]
        outs.append(jax.ShapeDtypeStruct((8, 128), jnp.float32))
        args.append(part)
        specs.append(vm)
    return pl.pallas_call(
        functools.partial(scatter_kernel, Z, J, n, sub, with_loss),
        out_shape=outs,
        in_specs=specs,
        out_specs=[vm] * len(outs),
        scratch_shapes=scratch,
        name=name,
        cost_estimate=pl.CostEstimate(
            flops=2 * rows * K * N, bytes_accessed=2 * (K * N + rows * K), transcendentals=0
        ),
        compiler_params=pltpu.CompilerParams(
            collective_id=cid, has_side_effects=True, vmem_limit_bytes=48 * 2**20
        ),
    )(*args)


def local(teacher_in, gate_weight, up_weight, down_weight, post_gain, student_in, proj_weight):
    width_count = lax.axis_size("tensor")
    own_sums = width_count == 16 and teacher_in.shape[0] % 16 == 0
    gains = post_gain.astype(jnp.float32)
    contract_last = (((1,), (1,)), ((), ()))
    block_rows = lax.all_gather(teacher_in, "tensor", axis=0, tiled=True)
    gate_value = lax.dot_general(
        block_rows, gate_weight, contract_last, preferred_element_type=jnp.float32
    )
    lift_value = lax.dot_general(
        block_rows, up_weight, contract_last, preferred_element_type=jnp.float32
    )
    hidden = (jax.nn.gelu(gate_value, approximate=True) * lift_value).astype(jnp.bfloat16)
    student_all = lax.all_gather(student_in, "tensor", axis=0, tiled=True)
    if own_sums:
        (ffn_out,) = scatter_matmul(
            hidden, down_weight, width_count, 768, 256, jnp.float32, "down_scatter", 1
        )
    else:
        ffn_out = lax.psum_scatter(
            jnp.dot(hidden, down_weight, preferred_element_type=jnp.float32),
            "tensor",
            scatter_dimension=0,
            tiled=True,
        )
    inv_norm = lax.rsqrt(jnp.mean(ffn_out * ffn_out, axis=-1, keepdims=True) + epsilon)
    target_rows = (teacher_in.astype(jnp.float32) + ffn_out * inv_norm * gains).astype(jnp.bfloat16)
    target = lax.all_to_all(target_rows, "tensor", split_axis=1, concat_axis=0, tiled=True)
    projected = lax.dot_general(
        student_all, proj_weight, contract_last, preferred_element_type=jnp.float32
    )
    difference = projected - target.astype(jnp.float32)
    squares = jnp.sum(difference * difference)
    cotangent = difference.astype(jnp.bfloat16)
    proj_grad = lax.dot_general(
        cotangent, student_all, (((0,), (0,)), ((), ())), preferred_element_type=jnp.float32
    )
    if own_sums:
        student_grad, total = scatter_matmul(
            cotangent, proj_weight, width_count, 512, 256, jnp.bfloat16, "grad_scatter", 2,
            jnp.full((8, 128), squares, jnp.float32),
        )
        total_error = total[0, 0]
    else:
        total_error = lax.psum(squares, "tensor")
        student_grad = lax.psum_scatter(
            jnp.dot(cotangent, proj_weight, preferred_element_type=jnp.float32),
            "tensor",
            scatter_dimension=0,
            tiled=True,
        ).astype(jnp.bfloat16)
    loss_value = total_error / (student_all.shape[0] * proj_weight.shape[0] * width_count)
    return (jnp.reshape(loss_value, (1,)), proj_grad, student_grad)


def solution(mesh):
    placed = (
        P(("groups", "tensor"), None),
        P("tensor", None),
        P("tensor", None),
        P("tensor", None),
        P(),
        P(("groups", "tensor"), None),
        P("tensor", None),
    )
    return jax.shard_map(
        local,
        mesh=mesh,
        in_specs=placed,
        out_specs=(P("groups"), P(("groups", "tensor"), None), P(("groups", "tensor"), None)),
        check_vma=False,
    )
```

```python
import functools

import jax
import jax.numpy as jnp
from jax import lax
from jax.experimental import pallas as pl
from jax.experimental.pallas import tpu as pltpu
from jax.sharding import PartitionSpec as P

epsilon = 1e-06
MESH = pl.DeviceIdType.MESH


def send(src, dst, send_sem, recv_sem, target):
    return pltpu.make_async_remote_copy(
        src_ref=src,
        dst_ref=dst,
        send_sem=send_sem,
        recv_sem=recv_sem,
        device_id={"tensor": target},
        device_id_type=MESH,
    )


def meet(targets):
    barrier = pltpu.get_barrier_semaphore()
    for target in targets:
        pl.semaphore_signal(barrier, inc=1, device_id={"tensor": target}, device_id_type=MESH)
    pl.semaphore_wait(barrier, len(targets))


def position(Z):
    me = lax.axis_index("tensor")
    c = lax.rem(me, 2)
    y = lax.rem(me // 2, 2)
    z = me // 4
    core = me + 1 - 2 * c
    across = me + 2 - 4 * y
    line = [lax.rem(z + k, Z) for k in range(1, Z)]
    return me, c, y, z, core, across, line


def scatter_kernel(Z, J, n, sub, with_loss, *refs):
    if with_loss:
        (lhs, w, part, out, total, wbuf, p, r1, s1, r2, s2, r3, wsem,
         cs, cr, ys, yr, zs, zr, heard, hs, hr) = refs
    else:
        (lhs, w, out, wbuf, p, r1, s1, r2, s2, r3, wsem, cs, cr, ys, yr, zs, zr) = refs
    f32 = jnp.float32
    me, c, y, z, core, across, line = position(Z)
    T = 4 * Z
    B = out.shape[0]

    def fetch(j):
        return pltpu.make_async_copy(w.at[:, pl.ds(j * n, n)], wbuf.at[j % 2], wsem.at[j % 2])

    fetch(0).start()
    others = [lax.rem(me + k, T) for k in range(1, T)]
    meet(others if with_loss else [core, across] + [v * 4 + y * 2 + c for v in line])
    notes = []
    if with_loss:
        for k in range(T - 1):
            notes.append(send(part, heard.at[k], hs.at[k], hr.at[k], others[k]))
            notes[-1].start()

    first = [send(p.at[j, :, :, 1 - c], r1.at[j], cs.at[j], cr.at[j], core) for j in range(J)]
    second = [send(s1.at[j], r2.at[j], ys.at[j], yr.at[j], across) for j in range(J)]
    third = [
        [
            send(s2.at[j, v], r3.at[j, k], zs.at[j, k], zr.at[j, k], v * 4 + y * 2 + c)
            for k, v in enumerate(line)
        ]
        for j in range(J)
    ]

    for t in range(J + 3):
        if t < J:
            fetch(t).wait()
            if t + 1 < J:
                fetch(t + 1).start()

            @pl.loop(0, n // sub)
            def _(i, t=t):
                cols = pl.ds(pl.multiple_of(i * sub, sub), sub)
                depth = lhs.shape[2]
                got = sum(
                    jnp.dot(
                        lhs[q], wbuf[t % 2, q * depth : (q + 1) * depth, cols],
                        preferred_element_type=f32,
                    )
                    for q in range(lhs.shape[0])
                )
                p[t, :, :, :, :, cols] = got.astype(jnp.bfloat16).reshape(Z, 2, 2, B, sub)

            first[t].start()
        j = t - 1
        if 0 <= j < J:
            first[j].wait_recv()
            s1[j] = (p[j, :, 1 - y, c].astype(f32) + r1[j, :, 1 - y].astype(f32)).astype(jnp.bfloat16)
            second[j].start()
        j = t - 2
        if 0 <= j < J:
            second[j].wait_recv()
            s2[j] = (
                p[j, :, y, c].astype(f32) + r1[j, :, y].astype(f32) + r2[j].astype(f32)
            ).astype(jnp.bfloat16)
            for copy in third[j]:
                copy.start()
        j = t - 3
        if 0 <= j < J:
            own = p[j, z, y, c].astype(f32) + r1[j, z, y].astype(f32) + r2[j, z].astype(f32)
            for k, copy in enumerate(third[j]):
                copy.wait_recv()
                own += r3[j, k].astype(f32)
            out[:, j * n : (j + 1) * n] = own.astype(out.dtype)
    for j in range(J):
        first[j].wait_send()
        second[j].wait_send()
        for copy in third[j]:
            copy.wait_send()
    if with_loss:
        acc = part[...]
        for k, copy in enumerate(notes):
            copy.wait()
            acc += heard[k]
        total[...] = acc


def gather_kernel(Z, J, n, S, m, G, x, st, gate, up, hidden, student, wbuf, xa, xs, acc,
                  wsem, zs, zr, ys, yr, cs, cr):
    f32 = jnp.float32
    me, c, y, z, core, across, line = position(Z)
    B = x.shape[0]
    R = 4 * Z * B
    g = gate.shape[0] // G

    def fetch(j):
        cols = pl.ds(j * n, n)
        return [
            pltpu.make_async_copy(w.at[:, cols], wbuf.at[i, j % 2], wsem.at[i, j % 2])
            for i, w in enumerate((gate, up))
        ]

    for j in range(min(2, J)):
        for copy in fetch(j):
            copy.start()
    for j in range(J):
        xa[j, z, y, c] = x[:, j * n : (j + 1) * n]
    for j in range(S):
        xs[j, z, y, c] = st[:, j * m : (j + 1) * m]
    targets = [v * 4 + y * 2 + c for v in line]
    meet([core, across] + targets)

    items = [xa.at[j] for j in range(J)] + [xs.at[j] for j in range(S)]
    first = [
        [
            send(a.at[z, y, c], a.at[z, y, c], zs.at[i, k], zr.at[i, k], v)
            for k, v in enumerate(targets)
        ]
        for i, a in enumerate(items)
    ]
    second = [
        send(a.at[:, y, c], a.at[:, y, c], ys.at[i], yr.at[i], across)
        for i, a in enumerate(items)
    ]
    third = [
        send(a.at[:, :, c], a.at[:, :, c], cs.at[i], cr.at[i], core)
        for i, a in enumerate(items)
    ]

    def multiply(j):
        for copy in fetch(j):
            copy.wait()

        @pl.loop(0, G)
        def _(i):
            rows = pl.ds(pl.multiple_of(i * g, 16), g)
            block = xa[j].reshape(R, n)
            got = []
            for which in range(2):
                d = lax.dot_general(
                    block, wbuf[which, j % 2, rows, :], (((1,), (1,)), ((), ())),
                    preferred_element_type=f32,
                )
                if j > 0:
                    d += acc[which, i]
                if j < J - 1:
                    acc[which, i] = d
                got.append(d)
            if j == J - 1:
                hidden[i] = (jax.nn.gelu(got[0], approximate=True) * got[1]).astype(jnp.bfloat16)

        if j + 2 < J:
            for copy in fetch(j + 2):
                copy.start()

    for t in range(J + S + 3):
        if t < J + S:
            for copy in first[t]:
                copy.start()
        if 0 <= t - 1 < J + S:
            for copy in first[t - 1]:
                copy.wait_recv()
            second[t - 1].start()
        if 0 <= t - 2 < J + S:
            second[t - 2].wait_recv()
            third[t - 2].start()
        if 0 <= t - 3 < J + S:
            third[t - 3].wait_recv()
            if t - 3 < J:
                multiply(t - 3)
            else:
                j = t - 3 - J
                student[:, j * m : (j + 1) * m] = xs[j].reshape(R, m)
    for i in range(J + S):
        for copy in first[i]:
            copy.wait_send()
        second[i].wait_send()
        third[i].wait_send()


def gather_ffn(x, st, gate, up, T, n, m, G, cid):
    Z = T // 4
    B, K = x.shape
    N = gate.shape[0]
    J, S = K // n, st.shape[1] // m
    bf = jnp.bfloat16
    V = pltpu.VMEM
    D = pltpu.SemaphoreType.DMA
    vm = pl.BlockSpec(memory_space=pltpu.VMEM)
    hbm = pl.BlockSpec(memory_space=pl.ANY)
    return pl.pallas_call(
        functools.partial(gather_kernel, Z, J, n, S, m, G),
        out_shape=[
            jax.ShapeDtypeStruct((G, T * B, N // G), bf),
            jax.ShapeDtypeStruct((T * B, st.shape[1]), bf),
        ],
        in_specs=[vm, vm, hbm, hbm],
        out_specs=[vm, vm],
        scratch_shapes=[
            V((2, 2, N, n), bf), V((J, Z, 2, 2, B, n), bf), V((S, Z, 2, 2, B, m), bf),
            V((2, G, T * B, N // G), jnp.float32), D((2, 2)),
            D((J + S, Z - 1)), D((J + S, Z - 1)), D((J + S,)), D((J + S,)), D((J + S,)), D((J + S,)),
        ],
        name="gather_ffn",
        cost_estimate=pl.CostEstimate(
            flops=4 * T * B * K * N, bytes_accessed=4 * K * N, transcendentals=0
        ),
        compiler_params=pltpu.CompilerParams(
            collective_id=cid, has_side_effects=True, vmem_limit_bytes=48 * 2**20
        ),
    )(x, st, gate, up)


def scatter_matmul(lhs, w, T, n, sub, dtype, name, cid, part=None):
    Z = T // 4
    rows = lhs.shape[1]
    K, N = w.shape
    J, B = N // n, rows // T
    bf = jnp.bfloat16
    V = pltpu.VMEM
    D = pltpu.SemaphoreType.DMA
    vm = pl.BlockSpec(memory_space=pltpu.VMEM)
    with_loss = part is not None
    scratch = [
        V((2, K, n), bf), V((J, Z, 2, 2, B, n), bf), V((J, Z, 2, B, n), bf), V((J, Z, B, n), bf),
        V((J, Z, B, n), bf), V((J, Z, B, n), bf), V((J, Z - 1, B, n), bf), D((2,)),
        D((J,)), D((J,)), D((J,)), D((J,)), D((J, Z - 1)), D((J, Z - 1)),
    ]
    outs = [jax.ShapeDtypeStruct((B, N), dtype)]
    args = [lhs, w]
    specs = [vm, pl.BlockSpec(memory_space=pl.ANY)]
    if with_loss:
        scratch += [V((T - 1, 8, 128), jnp.float32), D((T - 1,)), D((T - 1,))]
        outs.append(jax.ShapeDtypeStruct((8, 128), jnp.float32))
        args.append(part)
        specs.append(vm)
    return pl.pallas_call(
        functools.partial(scatter_kernel, Z, J, n, sub, with_loss),
        out_shape=outs,
        in_specs=specs,
        out_specs=[vm] * len(outs),
        scratch_shapes=scratch,
        name=name,
        cost_estimate=pl.CostEstimate(
            flops=2 * rows * K * N, bytes_accessed=2 * (K * N + rows * K), transcendentals=0
        ),
        compiler_params=pltpu.CompilerParams(
            collective_id=cid, has_side_effects=True, vmem_limit_bytes=48 * 2**20
        ),
    )(*args)


def local(teacher_in, gate_weight, up_weight, down_weight, post_gain, student_in, proj_weight):
    width_count = lax.axis_size("tensor")
    own_sums = width_count == 16 and teacher_in.shape[0] % 16 == 0
    gains = post_gain.astype(jnp.float32)
    contract_last = (((1,), (1,)), ((), ()))
    if own_sums:
        hidden, student_all = gather_ffn(
            teacher_in, student_in, gate_weight, up_weight, width_count, 768, 640, 6, 3
        )
    else:
        block_rows = lax.all_gather(teacher_in, "tensor", axis=0, tiled=True)
        gate_value = lax.dot_general(
            block_rows, gate_weight, contract_last, preferred_element_type=jnp.float32
        )
        lift_value = lax.dot_general(
            block_rows, up_weight, contract_last, preferred_element_type=jnp.float32
        )
        hidden = (jax.nn.gelu(gate_value, approximate=True) * lift_value).astype(jnp.bfloat16)
        student_all = lax.all_gather(student_in, "tensor", axis=0, tiled=True)
    if own_sums:
        (ffn_out,) = scatter_matmul(
            hidden, down_weight, width_count, 768, 256, jnp.float32, "down_scatter", 1
        )
    else:
        ffn_out = lax.psum_scatter(
            jnp.dot(hidden, down_weight, preferred_element_type=jnp.float32),
            "tensor",
            scatter_dimension=0,
            tiled=True,
        )
    inv_norm = lax.rsqrt(jnp.mean(ffn_out * ffn_out, axis=-1, keepdims=True) + epsilon)
    target_rows = (teacher_in.astype(jnp.float32) + ffn_out * inv_norm * gains).astype(jnp.bfloat16)
    target = lax.all_to_all(target_rows, "tensor", split_axis=1, concat_axis=0, tiled=True)
    projected = lax.dot_general(
        student_all, proj_weight, contract_last, preferred_element_type=jnp.float32
    )
    difference = projected - target.astype(jnp.float32)
    squares = jnp.sum(difference * difference)
    cotangent = difference.astype(jnp.bfloat16)
    proj_grad = lax.dot_general(
        cotangent, student_all, (((0,), (0,)), ((), ())), preferred_element_type=jnp.float32
    )
    if own_sums:
        student_grad, total = scatter_matmul(
            cotangent[None], proj_weight, width_count, 512, 256, jnp.bfloat16, "grad_scatter", 2,
            jnp.full((8, 128), squares, jnp.float32),
        )
        total_error = total[0, 0]
    else:
        total_error = lax.psum(squares, "tensor")
        student_grad = lax.psum_scatter(
            jnp.dot(cotangent, proj_weight, preferred_element_type=jnp.float32),
            "tensor",
            scatter_dimension=0,
            tiled=True,
        ).astype(jnp.bfloat16)
    loss_value = total_error / (student_all.shape[0] * proj_weight.shape[0] * width_count)
    return (jnp.reshape(loss_value, (1,)), proj_grad, student_grad)


def solution(mesh):
    placed = (
        P(("groups", "tensor"), None),
        P("tensor", None),
        P("tensor", None),
        P("tensor", None),
        P(),
        P(("groups", "tensor"), None),
        P("tensor", None),
    )
    return jax.shard_map(
        local,
        mesh=mesh,
        in_specs=placed,
        out_specs=(P("groups"), P(("groups", "tensor"), None), P(("groups", "tensor"), None)),
        check_vma=False,
    )
```

```python
import functools

import jax
import jax.numpy as jnp
from jax import lax
from jax.experimental import pallas as pl
from jax.experimental.pallas import tpu as pltpu
from jax.sharding import PartitionSpec as P

epsilon = 1e-06
lag = 2
MESH = pl.DeviceIdType.MESH


def send(src, dst, send_sem, recv_sem, target):
    return pltpu.make_async_remote_copy(
        src_ref=src,
        dst_ref=dst,
        send_sem=send_sem,
        recv_sem=recv_sem,
        device_id={"tensor": target},
        device_id_type=MESH,
    )


def meet(targets):
    barrier = pltpu.get_barrier_semaphore()
    for target in targets:
        pl.semaphore_signal(barrier, inc=1, device_id={"tensor": target}, device_id_type=MESH)
    pl.semaphore_wait(barrier, len(targets))


def position(Z):
    me = lax.axis_index("tensor")
    c = lax.rem(me, 2)
    y = lax.rem(me // 2, 2)
    z = me // 4
    core = me + 1 - 2 * c
    across = me + 2 - 4 * y
    line = [lax.rem(z + k, Z) for k in range(1, Z)]
    return me, c, y, z, core, across, line


def scatter_kernel(Z, J, n, sub, with_loss, *refs):
    if not with_loss:
        (lhs, w, x, gain, target, wbuf, p, r1, s1, r2, s2, r3, wsem,
         cs, cr, ys, yr, zs, zr, out, tb, tr, hs, hr) = refs
    else:
        (lhs, w, part, out, total, wbuf, p, r1, s1, r2, s2, r3, wsem,
         cs, cr, ys, yr, zs, zr, heard, hs, hr) = refs
    f32 = jnp.float32
    me, c, y, z, core, across, line = position(Z)
    T = 4 * Z
    B = out.shape[0]

    def fetch(j):
        return pltpu.make_async_copy(w.at[:, pl.ds(j * n, n)], wbuf.at[j % 2], wsem.at[j % 2])

    fetch(0).start()
    others = [lax.rem(me + k, T) for k in range(1, T)]
    meet(others)
    notes = []
    if with_loss:
        for k in range(T - 1):
            notes.append(send(part, heard.at[k], hs.at[k], hr.at[k], others[k]))
            notes[-1].start()

    first = [send(p.at[j, :, :, 1 - c], r1.at[j], cs.at[j], cr.at[j], core) for j in range(J)]
    second = [send(s1.at[j], r2.at[j], ys.at[j], yr.at[j], across) for j in range(J)]
    third = [
        [
            send(s2.at[j, v], r3.at[j, k], zs.at[j, k], zr.at[j, k], v * 4 + y * 2 + c)
            for k, v in enumerate(line)
        ]
        for j in range(J)
    ]

    for t in range(J + 2 * lag + 1):
        if t < J:
            fetch(t).wait()
            if t + 1 < J:
                fetch(t + 1).start()

            @pl.loop(0, n // sub)
            def _(i, t=t):
                cols = pl.ds(pl.multiple_of(i * sub, sub), sub)
                depth = lhs.shape[2]
                got = sum(
                    jnp.dot(
                        lhs[q], wbuf[t % 2, q * depth : (q + 1) * depth, cols],
                        preferred_element_type=f32,
                    )
                    for q in range(lhs.shape[0])
                )
                p[t, :, :, :, :, cols] = got.astype(jnp.bfloat16).reshape(Z, 2, 2, B, sub)

            first[t].start()
        j = t - 1
        if 0 <= j < J:
            first[j].wait_recv()
            s1[j] = (p[j, :, 1 - y, c].astype(f32) + r1[j, :, 1 - y].astype(f32)).astype(jnp.bfloat16)
            second[j].start()
        j = t - 1 - lag
        if 0 <= j < J:
            second[j].wait_recv()
            s2[j] = (
                p[j, :, y, c].astype(f32) + r1[j, :, y].astype(f32) + r2[j].astype(f32)
            ).astype(jnp.bfloat16)
            for copy in third[j]:
                copy.start()
        j = t - 1 - 2 * lag
        if 0 <= j < J:
            own = p[j, z, y, c].astype(f32) + r1[j, z, y].astype(f32) + r2[j, z].astype(f32)
            for k, copy in enumerate(third[j]):
                copy.wait_recv()
                own += r3[j, k].astype(f32)
            out[:, j * n : (j + 1) * n] = own.astype(out.dtype)
    if not with_loss:
        whole = out[...]
        inv_norm = lax.rsqrt(jnp.mean(whole * whole, axis=-1, keepdims=True) + epsilon)
        size = target.shape[1]
        for d in range(T):
            cols = slice(d * size, (d + 1) * size)
            tb[d] = (
                x[:, cols].astype(f32) + out[:, cols] * inv_norm * gain[:, cols].astype(f32)
            ).astype(jnp.bfloat16)
        for k, v in enumerate(others):
            notes.append(send(tb.at[v], tr.at[me], hs.at[k], hr.at[k], v))
            notes[-1].start()
        tr[me] = tb[me]
    for j in range(J):
        first[j].wait_send()
        second[j].wait_send()
        for copy in third[j]:
            copy.wait_send()
    if with_loss:
        acc = part[...]
        for k, copy in enumerate(notes):
            copy.wait()
            acc += heard[k]
        total[...] = acc
    else:
        for copy in notes:
            copy.wait()
        target[...] = tr[...].reshape(target.shape)


def gather_kernel(Z, J, n, S, m, G, x, st, gate, up, hidden, student, wbuf, xa, xs, acc,
                  wsem, zs, zr, ys, yr, cs, cr):
    f32 = jnp.float32
    me, c, y, z, core, across, line = position(Z)
    B = x.shape[0]
    R = 4 * Z * B
    g = gate.shape[0] // G

    def fetch(j):
        cols = pl.ds(j * n, n)
        return [
            pltpu.make_async_copy(w.at[:, cols], wbuf.at[i, j % 2], wsem.at[i, j % 2])
            for i, w in enumerate((gate, up))
        ]

    for j in range(min(2, J)):
        for copy in fetch(j):
            copy.start()
    for j in range(J):
        xa[j, z, y, c] = x[:, j * n : (j + 1) * n]
    for j in range(S):
        xs[j, z, y, c] = st[:, j * m : (j + 1) * m]
    targets = [v * 4 + y * 2 + c for v in line]
    meet([core, across] + targets)

    items = [xa.at[j] for j in range(J)] + [xs.at[j] for j in range(S)]
    first = [
        [
            send(a.at[z, y, c], a.at[z, y, c], zs.at[i, k], zr.at[i, k], v)
            for k, v in enumerate(targets)
        ]
        for i, a in enumerate(items)
    ]
    second = [
        send(a.at[:, y, c], a.at[:, y, c], ys.at[i], yr.at[i], across)
        for i, a in enumerate(items)
    ]
    third = [
        send(a.at[:, :, c], a.at[:, :, c], cs.at[i], cr.at[i], core)
        for i, a in enumerate(items)
    ]

    def multiply(j):
        for copy in fetch(j):
            copy.wait()

        @pl.loop(0, G)
        def _(i):
            rows = pl.ds(pl.multiple_of(i * g, 16), g)
            block = xa[j].reshape(R, n)
            got = []
            for which in range(2):
                d = lax.dot_general(
                    block, wbuf[which, j % 2, rows, :], (((1,), (1,)), ((), ())),
                    preferred_element_type=f32,
                )
                if j > 0:
                    d += acc[which, i]
                if j < J - 1:
                    acc[which, i] = d
                got.append(d)
            if j == J - 1:
                hidden[i] = (jax.nn.gelu(got[0], approximate=True) * got[1]).astype(jnp.bfloat16)

        if j + 2 < J:
            for copy in fetch(j + 2):
                copy.start()

    for t in range(J + S + 2 * lag + 1):
        if t < J + S:
            for copy in first[t]:
                copy.start()
        i = t - lag
        if 0 <= i < J + S:
            for copy in first[i]:
                copy.wait_recv()
            second[i].start()
        i = t - 2 * lag
        if 0 <= i < J + S:
            second[i].wait_recv()
            third[i].start()
        i = t - 2 * lag - 1
        if 0 <= i < J + S:
            third[i].wait_recv()
            if i < J:
                multiply(i)
            else:
                j = i - J
                student[:, j * m : (j + 1) * m] = xs[j].reshape(R, m)
    for i in range(J + S):
        for copy in first[i]:
            copy.wait_send()
        second[i].wait_send()
        third[i].wait_send()


def gather_ffn(x, st, gate, up, T, n, m, G, cid):
    Z = T // 4
    B, K = x.shape
    N = gate.shape[0]
    J, S = K // n, st.shape[1] // m
    bf = jnp.bfloat16
    V = pltpu.VMEM
    D = pltpu.SemaphoreType.DMA
    vm = pl.BlockSpec(memory_space=pltpu.VMEM)
    hbm = pl.BlockSpec(memory_space=pl.ANY)
    return pl.pallas_call(
        functools.partial(gather_kernel, Z, J, n, S, m, G),
        out_shape=[
            jax.ShapeDtypeStruct((G, T * B, N // G), bf),
            jax.ShapeDtypeStruct((T * B, st.shape[1]), bf),
        ],
        in_specs=[vm, vm, hbm, hbm],
        out_specs=[vm, vm],
        scratch_shapes=[
            V((2, 2, N, n), bf), V((J, Z, 2, 2, B, n), bf), V((S, Z, 2, 2, B, m), bf),
            V((2, G, T * B, N // G), jnp.float32), D((2, 2)),
            D((J + S, Z - 1)), D((J + S, Z - 1)), D((J + S,)), D((J + S,)), D((J + S,)), D((J + S,)),
        ],
        name="gather_ffn",
        cost_estimate=pl.CostEstimate(
            flops=4 * T * B * K * N, bytes_accessed=4 * K * N, transcendentals=0
        ),
        compiler_params=pltpu.CompilerParams(
            collective_id=cid, has_side_effects=True, vmem_limit_bytes=48 * 2**20
        ),
    )(x, st, gate, up)


def scatter_matmul(lhs, w, T, n, sub, name, cid, part=None, x=None, gain=None):
    Z = T // 4
    rows = lhs.shape[1]
    K, N = w.shape
    J, B = N // n, rows // T
    bf = jnp.bfloat16
    V = pltpu.VMEM
    D = pltpu.SemaphoreType.DMA
    vm = pl.BlockSpec(memory_space=pltpu.VMEM)
    with_loss = part is not None
    scratch = [
        V((2, K, n), bf), V((J, Z, 2, 2, B, n), bf), V((J, Z, 2, B, n), bf), V((J, Z, B, n), bf),
        V((J, Z, B, n), bf), V((J, Z, B, n), bf), V((J, Z - 1, B, n), bf), D((2,)),
        D((J,)), D((J,)), D((J,)), D((J,)), D((J, Z - 1)), D((J, Z - 1)),
    ]
    specs = [vm, pl.BlockSpec(memory_space=pl.ANY), vm]
    if with_loss:
        scratch += [V((T - 1, 8, 128), jnp.float32), D((T - 1,)), D((T - 1,))]
        outs = [jax.ShapeDtypeStruct((B, N), bf), jax.ShapeDtypeStruct((8, 128), jnp.float32)]
        args = [lhs, w, part]
    else:
        scratch += [V((B, N), jnp.float32), V((T, B, N // T), bf), V((T, B, N // T), bf)]
        scratch += [D((T - 1,)), D((T - 1,))]
        outs = [jax.ShapeDtypeStruct((rows, N // T), bf)]
        args = [lhs, w, x, gain]
        specs.append(vm)
    return pl.pallas_call(
        functools.partial(scatter_kernel, Z, J, n, sub, with_loss),
        out_shape=outs,
        in_specs=specs,
        out_specs=[vm] * len(outs),
        scratch_shapes=scratch,
        name=name,
        cost_estimate=pl.CostEstimate(
            flops=2 * rows * K * N, bytes_accessed=2 * (K * N + rows * K), transcendentals=0
        ),
        compiler_params=pltpu.CompilerParams(
            collective_id=cid, has_side_effects=True, vmem_limit_bytes=48 * 2**20
        ),
    )(*args)


def local(teacher_in, gate_weight, up_weight, down_weight, post_gain, student_in, proj_weight):
    width_count = lax.axis_size("tensor")
    own_sums = width_count == 16 and teacher_in.shape[0] % 16 == 0
    contract_last = (((1,), (1,)), ((), ()))
    if own_sums:
        hidden, student_all = gather_ffn(
            teacher_in, student_in, gate_weight, up_weight, width_count, 768, 640, 6, 3
        )
    else:
        block_rows = lax.all_gather(teacher_in, "tensor", axis=0, tiled=True)
        gate_value = lax.dot_general(
            block_rows, gate_weight, contract_last, preferred_element_type=jnp.float32
        )
        lift_value = lax.dot_general(
            block_rows, up_weight, contract_last, preferred_element_type=jnp.float32
        )
        hidden = (jax.nn.gelu(gate_value, approximate=True) * lift_value).astype(jnp.bfloat16)
        student_all = lax.all_gather(student_in, "tensor", axis=0, tiled=True)
    if own_sums:
        (target,) = scatter_matmul(
            hidden, down_weight, width_count, 384, 384, "down_scatter", 1,
            x=teacher_in, gain=post_gain[None],
        )
    else:
        ffn_out = lax.psum_scatter(
            jnp.dot(hidden, down_weight, preferred_element_type=jnp.float32),
            "tensor",
            scatter_dimension=0,
            tiled=True,
        )
        inv_norm = lax.rsqrt(jnp.mean(ffn_out * ffn_out, axis=-1, keepdims=True) + epsilon)
        target_rows = (
            teacher_in.astype(jnp.float32) + ffn_out * inv_norm * post_gain.astype(jnp.float32)
        ).astype(jnp.bfloat16)
        target = lax.all_to_all(target_rows, "tensor", split_axis=1, concat_axis=0, tiled=True)
    projected = lax.dot_general(
        student_all, proj_weight, contract_last, preferred_element_type=jnp.float32
    )
    difference = projected - target.astype(jnp.float32)
    squares = jnp.sum(difference * difference)
    cotangent = difference.astype(jnp.bfloat16)
    proj_grad = lax.dot_general(
        cotangent, student_all, (((0,), (0,)), ((), ())), preferred_element_type=jnp.float32
    )
    if own_sums:
        student_grad, total = scatter_matmul(
            cotangent[None], proj_weight, width_count, 256, 256, "grad_scatter", 2,
            part=jnp.full((8, 128), squares, jnp.float32),
        )
        total_error = total[0, 0]
    else:
        total_error = lax.psum(squares, "tensor")
        student_grad = lax.psum_scatter(
            jnp.dot(cotangent, proj_weight, preferred_element_type=jnp.float32),
            "tensor",
            scatter_dimension=0,
            tiled=True,
        ).astype(jnp.bfloat16)
    loss_value = total_error / (student_all.shape[0] * proj_weight.shape[0] * width_count)
    return (jnp.reshape(loss_value, (1,)), proj_grad, student_grad)


def solution(mesh):
    placed = (
        P(("groups", "tensor"), None),
        P("tensor", None),
        P("tensor", None),
        P("tensor", None),
        P(),
        P(("groups", "tensor"), None),
        P("tensor", None),
    )
    return jax.shard_map(
        local,
        mesh=mesh,
        in_specs=placed,
        out_specs=(P("groups"), P(("groups", "tensor"), None), P(("groups", "tensor"), None)),
        check_vma=False,
    )
```

```python
import functools

import jax
import jax.numpy as jnp
from jax import lax
from jax.experimental import pallas as pl
from jax.experimental.pallas import tpu as pltpu
from jax.sharding import PartitionSpec as P

epsilon = 1e-06
lag = 2
MESH = pl.DeviceIdType.MESH


def send(src, dst, send_sem, recv_sem, target):
    return pltpu.make_async_remote_copy(
        src_ref=src,
        dst_ref=dst,
        send_sem=send_sem,
        recv_sem=recv_sem,
        device_id={"tensor": target},
        device_id_type=MESH,
    )


def meet(targets):
    barrier = pltpu.get_barrier_semaphore()
    for target in targets:
        pl.semaphore_signal(barrier, inc=1, device_id={"tensor": target}, device_id_type=MESH)
    pl.semaphore_wait(barrier, len(targets))


def position(Z):
    me = lax.axis_index("tensor")
    c = lax.rem(me, 2)
    y = lax.rem(me // 2, 2)
    z = me // 4
    core = me + 1 - 2 * c
    across = me + 2 - 4 * y
    line = [lax.rem(z + k, Z) for k in range(1, Z)]
    return me, c, y, z, core, across, line


def scatter_kernel(Z, J, n, sub, with_loss, *refs):
    if not with_loss:
        (lhs, w, x, gain, target, wbuf, p, r1, s1, r2, s2, r3, wsem,
         cs, cr, ys, yr, zs, zr, out, tb, tr, hs, hr) = refs
    else:
        (lhs, w, part, out, total, wbuf, p, r1, s1, r2, s2, r3, wsem,
         cs, cr, ys, yr, zs, zr, heard, hs, hr) = refs
    f32 = jnp.float32
    me, c, y, z, core, across, line = position(Z)
    T = 4 * Z
    B = out.shape[0]

    def fetch(j):
        return pltpu.make_async_copy(w.at[:, pl.ds(j * n, n)], wbuf.at[j % 2], wsem.at[j % 2])

    fetch(0).start()
    others = [lax.rem(me + k, T) for k in range(1, T)]
    meet(others)
    notes = []
    if with_loss:
        for k in range(T - 1):
            notes.append(send(part, heard.at[k], hs.at[k], hr.at[k], others[k]))
            notes[-1].start()

    first = [send(p.at[j, :, :, 1 - c], r1.at[j], cs.at[j], cr.at[j], core) for j in range(J)]
    second = [send(s1.at[j], r2.at[j], ys.at[j], yr.at[j], across) for j in range(J)]
    third = [
        [
            send(s2.at[j, v], r3.at[j, k], zs.at[j, k], zr.at[j, k], v * 4 + y * 2 + c)
            for k, v in enumerate(line)
        ]
        for j in range(J)
    ]

    for t in range(J + 3):
        if t < J:
            fetch(t).wait()
            if t + 1 < J:
                fetch(t + 1).start()

            @pl.loop(0, n // sub)
            def _(i, t=t):
                cols = pl.ds(pl.multiple_of(i * sub, sub), sub)
                depth = lhs.shape[2]
                got = sum(
                    jnp.dot(
                        lhs[q], wbuf[t % 2, q * depth : (q + 1) * depth, cols],
                        preferred_element_type=f32,
                    )
                    for q in range(lhs.shape[0])
                )
                p[t, :, :, :, :, cols] = got.astype(jnp.bfloat16).reshape(Z, 2, 2, B, sub)

            first[t].start()
        j = t - 1
        if 0 <= j < J:
            first[j].wait_recv()
            s1[j] = (p[j, :, 1 - y, c].astype(f32) + r1[j, :, 1 - y].astype(f32)).astype(jnp.bfloat16)
            second[j].start()
        j = t - 2
        if 0 <= j < J:
            second[j].wait_recv()
            s2[j] = (
                p[j, :, y, c].astype(f32) + r1[j, :, y].astype(f32) + r2[j].astype(f32)
            ).astype(jnp.bfloat16)
            for copy in third[j]:
                copy.start()
        j = t - 3
        if 0 <= j < J:
            own = p[j, z, y, c].astype(f32) + r1[j, z, y].astype(f32) + r2[j, z].astype(f32)
            for k, copy in enumerate(third[j]):
                copy.wait_recv()
                own += r3[j, k].astype(f32)
            out[:, j * n : (j + 1) * n] = own.astype(out.dtype)
    if not with_loss:
        whole = out[...]
        inv_norm = lax.rsqrt(jnp.mean(whole * whole, axis=-1, keepdims=True) + epsilon)
        size = target.shape[1]
        for d in range(T):
            cols = slice(d * size, (d + 1) * size)
            tb[d] = (
                x[:, cols].astype(f32) + out[:, cols] * inv_norm * gain[:, cols].astype(f32)
            ).astype(jnp.bfloat16)
        for k, v in enumerate(others):
            notes.append(send(tb.at[v], tr.at[me], hs.at[k], hr.at[k], v))
            notes[-1].start()
        tr[me] = tb[me]
    for j in range(J):
        first[j].wait_send()
        second[j].wait_send()
        for copy in third[j]:
            copy.wait_send()
    if with_loss:
        acc = part[...]
        for k, copy in enumerate(notes):
            copy.wait()
            acc += heard[k]
        total[...] = acc
    else:
        for copy in notes:
            copy.wait()
        target[...] = tr[...].reshape(target.shape)


def gather_kernel(Z, J, n, S, m, G, x, st, gate, up, hidden, student, wbuf, xa, xs, acc,
                  wsem, zs, zr, ys, yr, cs, cr):
    f32 = jnp.float32
    me, c, y, z, core, across, line = position(Z)
    B = x.shape[0]
    R = 4 * Z * B
    g = gate.shape[0] // G

    def fetch(j):
        cols = pl.ds(j * n, n)
        return [
            pltpu.make_async_copy(w.at[:, cols], wbuf.at[i, j % 2], wsem.at[i, j % 2])
            for i, w in enumerate((gate, up))
        ]

    for j in range(min(2, J)):
        for copy in fetch(j):
            copy.start()
    for j in range(J):
        xa[j, z, y, c] = x[:, j * n : (j + 1) * n]
    for j in range(S):
        xs[j, z, y, c] = st[:, j * m : (j + 1) * m]
    targets = [v * 4 + y * 2 + c for v in line]
    meet([core, across] + targets)

    items = [xa.at[j] for j in range(J)] + [xs.at[j] for j in range(S)]
    first = [
        [
            send(a.at[z, y, c], a.at[z, y, c], zs.at[i, k], zr.at[i, k], v)
            for k, v in enumerate(targets)
        ]
        for i, a in enumerate(items)
    ]
    second = [
        send(a.at[:, y, c], a.at[:, y, c], ys.at[i], yr.at[i], across)
        for i, a in enumerate(items)
    ]
    third = [
        [
            send(a.at[:, v, c], a.at[:, v, c], cs.at[i, k], cr.at[i, k], core)
            for k, v in enumerate((y, 1 - y))
        ]
        for i, a in enumerate(items)
    ]

    def multiply(j):
        for copy in fetch(j):
            copy.wait()

        @pl.loop(0, G)
        def _(i):
            rows = pl.ds(pl.multiple_of(i * g, 16), g)
            block = xa[j].reshape(R, n)
            got = []
            for which in range(2):
                d = lax.dot_general(
                    block, wbuf[which, j % 2, rows, :], (((1,), (1,)), ((), ())),
                    preferred_element_type=f32,
                )
                if j > 0:
                    d += acc[which, i]
                if j < J - 1:
                    acc[which, i] = d
                got.append(d)
            if j == J - 1:
                hidden[i] = (jax.nn.gelu(got[0], approximate=True) * got[1]).astype(jnp.bfloat16)

        if j + 2 < J:
            for copy in fetch(j + 2):
                copy.start()

    for t in range(J + S + 2 * lag + 1):
        if t < J + S:
            for copy in first[t]:
                copy.start()
        i = t - lag
        if 0 <= i < J + S:
            for copy in first[i]:
                copy.wait_recv()
            second[i].start()
            third[i][0].start()
        i = t - 2 * lag
        if 0 <= i < J + S:
            second[i].wait_recv()
            third[i][1].start()
        i = t - 2 * lag - 1
        if 0 <= i < J + S:
            for copy in third[i]:
                copy.wait_recv()
            if i < J:
                multiply(i)
            else:
                j = i - J
                student[:, j * m : (j + 1) * m] = xs[j].reshape(R, m)
    for i in range(J + S):
        for copy in first[i]:
            copy.wait_send()
        second[i].wait_send()
        for copy in third[i]:
            copy.wait_send()


def gather_ffn(x, st, gate, up, T, n, m, G, cid):
    Z = T // 4
    B, K = x.shape
    N = gate.shape[0]
    J, S = K // n, st.shape[1] // m
    bf = jnp.bfloat16
    V = pltpu.VMEM
    D = pltpu.SemaphoreType.DMA
    vm = pl.BlockSpec(memory_space=pltpu.VMEM)
    hbm = pl.BlockSpec(memory_space=pl.ANY)
    return pl.pallas_call(
        functools.partial(gather_kernel, Z, J, n, S, m, G),
        out_shape=[
            jax.ShapeDtypeStruct((G, T * B, N // G), bf),
            jax.ShapeDtypeStruct((T * B, st.shape[1]), bf),
        ],
        in_specs=[vm, vm, hbm, hbm],
        out_specs=[vm, vm],
        scratch_shapes=[
            V((2, 2, N, n), bf), V((J, Z, 2, 2, B, n), bf), V((S, Z, 2, 2, B, m), bf),
            V((2, G, T * B, N // G), jnp.float32), D((2, 2)),
            D((J + S, Z - 1)), D((J + S, Z - 1)), D((J + S,)), D((J + S,)), D((J + S, 2)), D((J + S, 2)),
        ],
        name="gather_ffn",
        cost_estimate=pl.CostEstimate(
            flops=4 * T * B * K * N, bytes_accessed=4 * K * N, transcendentals=0
        ),
        compiler_params=pltpu.CompilerParams(
            collective_id=cid, has_side_effects=True, vmem_limit_bytes=48 * 2**20
        ),
    )(x, st, gate, up)


def scatter_matmul(lhs, w, T, n, sub, name, cid, part=None, x=None, gain=None):
    Z = T // 4
    rows = lhs.shape[1]
    K, N = w.shape
    J, B = N // n, rows // T
    bf = jnp.bfloat16
    V = pltpu.VMEM
    D = pltpu.SemaphoreType.DMA
    vm = pl.BlockSpec(memory_space=pltpu.VMEM)
    with_loss = part is not None
    scratch = [
        V((2, K, n), bf), V((J, Z, 2, 2, B, n), bf), V((J, Z, 2, B, n), bf), V((J, Z, B, n), bf),
        V((J, Z, B, n), bf), V((J, Z, B, n), bf), V((J, Z - 1, B, n), bf), D((2,)),
        D((J,)), D((J,)), D((J,)), D((J,)), D((J, Z - 1)), D((J, Z - 1)),
    ]
    specs = [vm, pl.BlockSpec(memory_space=pl.ANY), vm]
    if with_loss:
        scratch += [V((T - 1, 8, 128), jnp.float32), D((T - 1,)), D((T - 1,))]
        outs = [jax.ShapeDtypeStruct((B, N), bf), jax.ShapeDtypeStruct((8, 128), jnp.float32)]
        args = [lhs, w, part]
    else:
        scratch += [V((B, N), jnp.float32), V((T, B, N // T), bf), V((T, B, N // T), bf)]
        scratch += [D((T - 1,)), D((T - 1,))]
        outs = [jax.ShapeDtypeStruct((rows, N // T), bf)]
        args = [lhs, w, x, gain]
        specs.append(vm)
    return pl.pallas_call(
        functools.partial(scatter_kernel, Z, J, n, sub, with_loss),
        out_shape=outs,
        in_specs=specs,
        out_specs=[vm] * len(outs),
        scratch_shapes=scratch,
        name=name,
        cost_estimate=pl.CostEstimate(
            flops=2 * rows * K * N, bytes_accessed=2 * (K * N + rows * K), transcendentals=0
        ),
        compiler_params=pltpu.CompilerParams(
            collective_id=cid, has_side_effects=True, vmem_limit_bytes=48 * 2**20
        ),
    )(*args)


def local(teacher_in, gate_weight, up_weight, down_weight, post_gain, student_in, proj_weight):
    width_count = lax.axis_size("tensor")
    own_sums = width_count == 16 and teacher_in.shape[0] % 16 == 0
    contract_last = (((1,), (1,)), ((), ()))
    if own_sums:
        hidden, student_all = gather_ffn(
            teacher_in, student_in, gate_weight, up_weight, width_count, 768, 640, 6, 3
        )
    else:
        block_rows = lax.all_gather(teacher_in, "tensor", axis=0, tiled=True)
        gate_value = lax.dot_general(
            block_rows, gate_weight, contract_last, preferred_element_type=jnp.float32
        )
        lift_value = lax.dot_general(
            block_rows, up_weight, contract_last, preferred_element_type=jnp.float32
        )
        hidden = (jax.nn.gelu(gate_value, approximate=True) * lift_value).astype(jnp.bfloat16)
        student_all = lax.all_gather(student_in, "tensor", axis=0, tiled=True)
    if own_sums:
        (target,) = scatter_matmul(
            hidden, down_weight, width_count, 384, 384, "down_scatter", 1,
            x=teacher_in, gain=post_gain[None],
        )
    else:
        ffn_out = lax.psum_scatter(
            jnp.dot(hidden, down_weight, preferred_element_type=jnp.float32),
            "tensor",
            scatter_dimension=0,
            tiled=True,
        )
        inv_norm = lax.rsqrt(jnp.mean(ffn_out * ffn_out, axis=-1, keepdims=True) + epsilon)
        target_rows = (
            teacher_in.astype(jnp.float32) + ffn_out * inv_norm * post_gain.astype(jnp.float32)
        ).astype(jnp.bfloat16)
        target = lax.all_to_all(target_rows, "tensor", split_axis=1, concat_axis=0, tiled=True)
    projected = lax.dot_general(
        student_all, proj_weight, contract_last, preferred_element_type=jnp.float32
    )
    difference = projected - target.astype(jnp.float32)
    squares = jnp.sum(difference * difference)
    cotangent = difference.astype(jnp.bfloat16)
    proj_grad = lax.dot_general(
        cotangent, student_all, (((0,), (0,)), ((), ())), preferred_element_type=jnp.float32
    )
    if own_sums:
        student_grad, total = scatter_matmul(
            cotangent[None], proj_weight, width_count, 512, 256, "grad_scatter", 2,
            part=jnp.full((8, 128), squares, jnp.float32),
        )
        total_error = total[0, 0]
    else:
        total_error = lax.psum(squares, "tensor")
        student_grad = lax.psum_scatter(
            jnp.dot(cotangent, proj_weight, preferred_element_type=jnp.float32),
            "tensor",
            scatter_dimension=0,
            tiled=True,
        ).astype(jnp.bfloat16)
    loss_value = total_error / (student_all.shape[0] * proj_weight.shape[0] * width_count)
    return (jnp.reshape(loss_value, (1,)), proj_grad, student_grad)


def solution(mesh):
    placed = (
        P(("groups", "tensor"), None),
        P("tensor", None),
        P("tensor", None),
        P("tensor", None),
        P(),
        P(("groups", "tensor"), None),
        P("tensor", None),
    )
    return jax.shard_map(
        local,
        mesh=mesh,
        in_specs=placed,
        out_specs=(P("groups"), P(("groups", "tensor"), None), P(("groups", "tensor"), None)),
        check_vma=False,
    )
```
